512 devices in a mesh: head: 8 (over x, core), blk: 64 (over y, z).
Axes of the slice: x: 4, y: 8, z: 8, core: 2. Of those that a mesh axis runs over, the one named last changes fastest.
Arguments:
- suffix_hidden: bfloat16 [1536, 2048], P('blk'), may hold values from -400 to 400
- prefix_hidden: bfloat16 [16384, 2048], P('blk'), may hold values from -400 to 400
- kv_cache: bfloat16 [2, 16384, 8, 256], P(None, 'blk', 'head'), may hold values from -300 to 300
- norm_gain: float32 [2048], replicated, may hold values from 0.1 to 1.9
- norm_bias: float32 [2048], replicated, may hold values from -3 to 3
- qkv_weight: bfloat16 [2048, 8, 768], P('blk', 'head'), may hold values from -0.125 to 0.125
- qkv_bias: float32 [8, 768], P('head'), may hold values from -3 to 3
- out_weight: bfloat16 [8, 256, 2048], P('head', 'blk'), may hold values from -0.125 to 0.125
- out_bias: float32 [2048], replicated, may hold values from -3 to 3
- suffix_lengths: int32 [4], replicated, may hold values from 1 to 768, 1536 in all
- prefix_blocks: int32 [4], replicated, may hold values from 1 to 32, 64 in all
- block_owner: int32 [64], replicated, may hold values from 0 to 63, each once
- recompute_flag: int32 [16384], P('blk'), may hold values from 0 to 1, as said below
Outputs:
- attn_out: bfloat16 [1536, 2048], P('blk', 'head')
The draws below stay inside these ranges and needn't reach their ends.
Inputs may be any that keep to these rules, and one draw needn't show every extreme that they name: `recompute_flag`: each storage block of 256 cache rows holds exactly 25 ones.
All inputs are finite; a program needn't handle non-finite values.
Results may differ from the reference program's by a relative error of at most 0.015.
Values may be sent and summed in bfloat16 or wider, within the bound.
A program may use at most 64 MiB of HBM per device.

```python
import math
import jax
import jax.numpy as jnp
import numpy as np
from jax import lax

D = 2048
HEADS = 8
HEAD_DIM = 256
TENANTS = 4
SUF_DEV = 24
BLK_ROWS = 256
FLAG_DEV = 25
SUFFIX = 1536
CACHE = 16384
N_BLK = 64


def scaled_states(key, row_total):
    row_key, col_key, entry_key = jax.random.split(key, 3)
    row_scale = jnp.exp(jax.random.uniform(row_key, (row_total, 1), jnp.float32, 0.0, 2.302585))
    col_scale = jnp.exp(jax.random.uniform(col_key, (1, D), jnp.float32, 0.0, 2.302585))
    sampled = jnp.clip(jax.random.normal(entry_key, (row_total, D), jnp.float32), -4.0, 4.0)
    return sampled * row_scale * col_scale


def draw_suffix_hidden(key, part):
    return scaled_states(jax.random.fold_in(key, 11), SUFFIX).astype(jnp.bfloat16)


def draw_prefix_hidden(key, part):
    return scaled_states(jax.random.fold_in(key, 23), CACHE).astype(jnp.bfloat16)


def draw_kv_cache(key, part):
    streams = jax.random.split(jax.random.fold_in(key, 37), 3)
    cube_shape = (CACHE, HEADS, HEAD_DIM)
    stored_keys = jnp.clip(jax.random.normal(streams[1], cube_shape, jnp.float32), -4.0, 4.0)
    stored_values = jnp.clip(jax.random.normal(streams[2], cube_shape, jnp.float32), -4.0, 4.0)
    return jnp.stack([stored_keys, stored_values]).astype(jnp.bfloat16)


def draw_recompute_flag(key, part):
    block_total = CACHE // BLK_ROWS

    def draw_block(block_index):
        shuffled = jax.random.permutation(jax.random.fold_in(key, block_index), BLK_ROWS)
        return (shuffled < FLAG_DEV).astype(jnp.int32)
    return jax.vmap(draw_block)(jnp.arange(block_total, dtype=jnp.int32)).reshape(CACHE)


def block_levels(key, extent, cuts, least, top_value):
    level = 1.0
    for dim, shards_of in cuts:
        heights = jax.random.uniform(jax.random.fold_in(jax.random.fold_in(key, 6), dim), (shards_of,), jnp.float32, least / len(cuts), top_value / len(cuts))
        level = level * jnp.repeat(jnp.exp(heights), extent[dim] // shards_of).reshape((-1,) + (1,) * (len(extent) - 1 - dim))
    return level


def split_up(number_of, total, bound, lean):
    weights = [(1 << 20) // math.isqrt(rank ** lean) + 1 for rank in range(2, number_of + 1)]
    surplus, holding = total - bound - (number_of - 1), [1] * (number_of - 1)
    while surplus > 0:
        candidates = [i for i in range(number_of - 1) if holding[i] < bound]
        pool, remaining = sum([weights[i] for i in candidates]), surplus
        for i in candidates:
            extra = min(bound - holding[i], max(1, remaining * weights[i] // pool), surplus)
            holding[i] = holding[i] + extra
            surplus = surplus - extra
    return np.array([bound] + holding)


def uneven(stream_key, amount, total, limit, slope):
    if amount == 2:
        one = jax.random.randint(stream_key, (), max(1, total - limit), min(limit, total - 1) + 1)
        return jnp.stack([one, total - one])
    sizes = jnp.asarray(split_up(amount, total, limit, slope), jnp.int32)
    twos = (amount - 1) // 2
    donor, sink = sizes[1:1 + 2 * twos:2], sizes[2:2 + 2 * twos:2]
    slack = jnp.minimum(donor - 1, limit - sink)
    moved = jax.random.randint(jax.random.fold_in(stream_key, 1), (twos,), 0, 1 << 20) % (slack + 1)
    sizes = sizes.at[1:1 + 2 * twos:2].set(donor - moved).at[2:2 + 2 * twos:2].set(sink + moved)
    return sizes[jax.random.permutation(jax.random.fold_in(stream_key, 2), amount)]


def scatter_about(key, shape, deviation, limit, cuts=(), kind=jnp.bfloat16):
    array = jax.random.normal(key, shape, jnp.float32) * deviation
    if len(cuts) > 0:
        array = block_levels(key, shape, cuts, -0.22, 0.18) * array
    return jnp.clip(array, min=-limit, max=limit).astype(kind)


def setup_inputs(seed: int = 0) -> dict:
    arg_keys = jax.random.split(jax.random.key(seed), 14)
    suffix_hidden = draw_suffix_hidden(jax.random.fold_in(arg_keys[13], 71), 0)
    prefix_hidden = draw_prefix_hidden(jax.random.fold_in(arg_keys[13], 71), 0)
    kv_cache = draw_kv_cache(jax.random.fold_in(arg_keys[13], 71), 0)
    norm_gain = jnp.clip(1.0 + 0.18 * jax.random.normal(arg_keys[3], (D,), jnp.float32), 0.1, 1.9)
    norm_bias = scatter_about(arg_keys[4], (D,), 0.5, 3.0, (), jnp.float32)
    qkv_weight = scatter_about(arg_keys[5], (D, HEADS, 3 * HEAD_DIM), D ** -0.5, 0.125, ((0, 64), (1, 8)))
    qkv_bias = scatter_about(arg_keys[6], (HEADS, 3 * HEAD_DIM), 0.5, 3.0, ((0, 8),), jnp.float32)
    out_weight = scatter_about(arg_keys[7], (HEADS, HEAD_DIM, D), (HEADS * HEAD_DIM) ** -0.5, 0.125, ((0, 8), (1, 64)))
    out_bias = scatter_about(arg_keys[8], (D,), 0.5, 3.0, (), jnp.float32)
    suffix_lengths = uneven(arg_keys[9], TENANTS, SUFFIX, SUFFIX // 2, 2).astype(jnp.int32)
    prefix_blocks = uneven(arg_keys[10], TENANTS, N_BLK, N_BLK // 2, 2).astype(jnp.int32)
    block_owner = jax.random.permutation(arg_keys[11], N_BLK).astype(jnp.int32)
    recompute_flag = draw_recompute_flag(jax.random.fold_in(arg_keys[13], 71), 0)
    return {"suffix_hidden": suffix_hidden, "prefix_hidden": prefix_hidden, "kv_cache": kv_cache, "norm_gain": norm_gain, "norm_bias": norm_bias, "qkv_weight": qkv_weight, "qkv_bias": qkv_bias, "out_weight": out_weight, "out_bias": out_bias, "suffix_lengths": suffix_lengths, "prefix_blocks": prefix_blocks, "block_owner": block_owner, "recompute_flag": recompute_flag}


EPSILON = 1e-05
MASKED = -1e+30

def layer_norm(states, norm_scale, norm_shift):
    widened = states.astype(jnp.float32)
    average = lax.optimization_barrier(jnp.mean(widened, axis=-1, keepdims=True))
    center = widened - average
    variance = lax.optimization_barrier(jnp.mean(center * center, axis=-1, keepdims=True))
    return (center * lax.rsqrt(variance + EPSILON) * norm_scale + norm_shift).astype(jnp.bfloat16)

def tenant_of(bounds, positions):
    return lax.optimization_barrier(jnp.sum((positions[:, None] >= bounds[None, :]).astype(jnp.int32), axis=1)).astype(jnp.int32)

def absorb(running, offset, query_win, allowed, keys_blk, values_blk):
    best, denominator, accum = running
    win_rows = query_win.shape[0]
    old_best = lax.dynamic_slice_in_dim(best, offset, win_rows, 0)
    old_den = lax.dynamic_slice_in_dim(denominator, offset, win_rows, 0)
    old_acc = lax.dynamic_slice_in_dim(accum, offset, win_rows, 0)
    scores = jnp.einsum('whd,khd->whk', query_win.astype(jnp.float32), keys_blk.astype(jnp.float32)) * HEAD_DIM ** (-0.5)
    gate = allowed[:, None, :]
    block_best = lax.optimization_barrier(jnp.max(jnp.where(gate, scores, MASKED), axis=2))
    new_best = jnp.maximum(old_best, block_best)
    weights = jnp.where(gate, jnp.exp(scores - new_best[:, :, None]), 0.0)
    rounded = lax.optimization_barrier(weights.astype(jnp.bfloat16)).astype(jnp.float32)
    rescale = jnp.exp(old_best - new_best)
    new_den = old_den * rescale + lax.optimization_barrier(jnp.sum(weights, axis=2))
    new_acc = old_acc * rescale[:, :, None] + jnp.einsum('whk,khd->whd', rounded, values_blk.astype(jnp.float32))
    best = lax.dynamic_update_slice_in_dim(best, new_best, offset, 0)
    denominator = lax.dynamic_update_slice_in_dim(denominator, new_den, offset, 0)
    accum = lax.dynamic_update_slice_in_dim(accum, new_acc, offset, 0)
    return (best, denominator, accum)

def reference(suffix_hidden, prefix_hidden, kv_cache, norm_gain, norm_bias, qkv_weight, qkv_bias, out_weight, out_bias, suffix_lengths, prefix_blocks, block_owner, recompute_flag):
    normed = layer_norm(suffix_hidden, norm_gain, norm_bias)
    weight_flat = qkv_weight.reshape(D, HEADS * 3 * HEAD_DIM)
    projected = (jnp.dot(normed, weight_flat, preferred_element_type=jnp.float32) + qkv_bias.reshape(-1)).astype(jnp.bfloat16)
    projected = projected.reshape(SUFFIX, HEADS, 3 * HEAD_DIM)
    queries = projected[:, :, :HEAD_DIM]
    keys_new = projected[:, :, HEAD_DIM:2 * HEAD_DIM]
    values_new = projected[:, :, 2 * HEAD_DIM:]
    flagged = jnp.argsort(1 - recompute_flag, stable=True)[:FLAG_DEV * N_BLK].astype(jnp.int32)
    prefix_normed = layer_norm(prefix_hidden[flagged], norm_gain, norm_bias)
    kv_weight = qkv_weight[:, :, HEAD_DIM:].reshape(D, HEADS * 2 * HEAD_DIM)
    kv_shift = qkv_bias[:, HEAD_DIM:].reshape(-1)
    recomputed = (jnp.dot(prefix_normed, kv_weight, preferred_element_type=jnp.float32) + kv_shift).astype(jnp.bfloat16)
    recomputed = recomputed.reshape(FLAG_DEV * N_BLK, HEADS, 2 * HEAD_DIM)
    prefix_keys = kv_cache[0].at[flagged].set(recomputed[:, :, :HEAD_DIM])
    prefix_values = kv_cache[1].at[flagged].set(recomputed[:, :, HEAD_DIM:])
    tenant_ends = jnp.cumsum(suffix_lengths).astype(jnp.int32)
    tenant_starts = (tenant_ends - suffix_lengths).astype(jnp.int32)
    row_tenant = tenant_of(tenant_ends, jnp.arange(SUFFIX, dtype=jnp.int32))
    block_ends = jnp.cumsum(prefix_blocks).astype(jnp.int32)
    global_tenant = tenant_of(block_ends, jnp.arange(N_BLK, dtype=jnp.int32))
    block_tenant = jnp.zeros((N_BLK,), jnp.int32).at[block_owner].set(global_tenant)
    running = (jnp.full((SUFFIX, HEADS), MASKED, jnp.float32), jnp.zeros((SUFFIX, HEADS), jnp.float32), jnp.zeros((SUFFIX, HEADS, HEAD_DIM), jnp.float32))
    win_prefix = SUFFIX // 2
    win_suffix = min(SUFFIX, SUFFIX // 2 + SUF_DEV)

    def prefix_step(state, block_index):
        tenant = block_tenant[block_index]
        offset = jnp.minimum(tenant_starts[tenant], SUFFIX - win_prefix).astype(jnp.int32)
        query_win = lax.dynamic_slice_in_dim(queries, offset, win_prefix, 0)
        win_tenant = lax.dynamic_slice_in_dim(row_tenant, offset, win_prefix, 0)
        allowed = jnp.broadcast_to((win_tenant == tenant)[:, None], (win_prefix, BLK_ROWS))
        keys_blk = lax.dynamic_slice_in_dim(prefix_keys, (block_index * BLK_ROWS).astype(jnp.int32), BLK_ROWS, 0)
        values_blk = lax.dynamic_slice_in_dim(prefix_values, (block_index * BLK_ROWS).astype(jnp.int32), BLK_ROWS, 0)
        return (absorb(state, offset, query_win, allowed, keys_blk, values_blk), None)
    running, _ = lax.scan(prefix_step, running, jnp.arange(N_BLK, dtype=jnp.int32))

    def suffix_step(state, slab_index):
        key_first = (slab_index * SUF_DEV).astype(jnp.int32)
        offset = jnp.minimum(key_first, SUFFIX - win_suffix).astype(jnp.int32)
        query_win = lax.dynamic_slice_in_dim(queries, offset, win_suffix, 0)
        query_rows = offset + jnp.arange(win_suffix, dtype=jnp.int32)
        key_rows = key_first + jnp.arange(SUF_DEV, dtype=jnp.int32)
        query_tenant = lax.dynamic_slice_in_dim(row_tenant, offset, win_suffix, 0)
        key_tenant = lax.dynamic_slice_in_dim(row_tenant, key_first, SUF_DEV, 0)
        allowed = (query_tenant[:, None] == key_tenant[None, :]) & (key_rows[None, :] <= query_rows[:, None])
        keys_blk = lax.dynamic_slice_in_dim(keys_new, key_first, SUF_DEV, 0)
        values_blk = lax.dynamic_slice_in_dim(values_new, key_first, SUF_DEV, 0)
        return (absorb(state, offset, query_win, allowed, keys_blk, values_blk), None)
    running, _ = lax.scan(suffix_step, running, jnp.arange(N_BLK, dtype=jnp.int32))
    best, denominator, accum = running
    attended = (accum / denominator[:, :, None]).astype(jnp.bfloat16).reshape(SUFFIX, HEADS * HEAD_DIM)
    mixed = jnp.dot(attended, out_weight.reshape(HEADS * HEAD_DIM, D), preferred_element_type=jnp.float32)
    return (mixed + out_bias).astype(jnp.bfloat16)
```

```python
import math

import jax
import jax.numpy as jnp
from jax import lax
from jax.sharding import PartitionSpec as P

FLAG_DEV = 25


EPSILON = 1e-05
MASKED = -1e30


def layer_norm(states, norm_scale, norm_shift):
    widened = states.astype(jnp.float32)
    average = jnp.mean(widened, axis=-1, keepdims=True)
    center = widened - average
    variance = jnp.mean(center * center, axis=-1, keepdims=True)
    return (center * lax.rsqrt(variance + EPSILON) * norm_scale + norm_shift).astype(jnp.bfloat16)


def body(
    suffix_hidden,
    prefix_hidden,
    kv_cache,
    norm_gain,
    norm_bias,
    qkv_weight,
    qkv_bias,
    out_weight,
    out_bias,
    suffix_lengths,
    prefix_blocks,
    block_owner,
    recompute_flag,
):
    blk_total = lax.axis_size("blk")
    own_index = lax.axis_index("blk")
    row_count = suffix_hidden.shape[0]
    cache_rows = prefix_hidden.shape[0]
    heads_dev = qkv_weight.shape[1]
    head_dim = qkv_weight.shape[2] // 3
    total_rows = row_count * blk_total
    own_first = own_index * row_count
    tenant_ends = jnp.cumsum(suffix_lengths)
    row_ids = jnp.arange(total_rows, dtype=jnp.int32)
    row_tenant = jnp.sum((row_ids[:, None] >= tenant_ends[None, :]).astype(jnp.int32), axis=1)
    block_ends = jnp.cumsum(prefix_blocks)
    block_slots = jnp.arange(blk_total, dtype=jnp.int32)
    global_block = jnp.sum(jnp.where(block_owner == own_index, block_slots, 0))
    block_tenant = jnp.sum((global_block >= block_ends).astype(jnp.int32))
    normed = layer_norm(suffix_hidden, norm_gain, norm_bias)
    flagged = jnp.argsort(1 - recompute_flag, stable=True)[:FLAG_DEV]
    prefix_normed = layer_norm(prefix_hidden[flagged], norm_gain, norm_bias)
    qkv_rows = qkv_weight.shape[0]
    out_rows = out_weight.shape[1]
    model_dim = out_weight.shape[2]
    packed_weights = jnp.concatenate(
        [qkv_weight.reshape(1, -1), out_weight.reshape(1, -1)], axis=1
    )
    fetched_all = lax.all_gather(packed_weights, "blk", axis=0, tiled=True)
    qkv_size = qkv_rows * heads_dev * 3 * head_dim
    fetched = fetched_all[:, :qkv_size].reshape(blk_total * qkv_rows, heads_dev, 3 * head_dim)
    out_fetched = fetched_all[:, qkv_size:].reshape(blk_total, heads_dev, out_rows, model_dim)
    out_fetched = jnp.transpose(out_fetched, (1, 0, 2, 3)).reshape(
        heads_dev, blk_total * out_rows, model_dim
    )
    piece_rows = fetched.shape[0]
    flattened = fetched.reshape(piece_rows, heads_dev * 3 * head_dim)
    kv_part = fetched[:, :, head_dim:].reshape(piece_rows, heads_dev * 2 * head_dim)
    suffix_acc = jnp.dot(normed, flattened, preferred_element_type=jnp.float32)
    prefix_acc = jnp.dot(prefix_normed, kv_part, preferred_element_type=jnp.float32)
    suffix_acc, prefix_acc = (suffix_acc, prefix_acc)
    projected = (
        (suffix_acc + qkv_bias.reshape(-1))
        .astype(jnp.bfloat16)
        .reshape(row_count, heads_dev, 3 * head_dim)
    )
    recomputed = (
        (prefix_acc + qkv_bias[:, head_dim:].reshape(-1))
        .astype(jnp.bfloat16)
        .reshape(FLAG_DEV, heads_dev, 2 * head_dim)
    )
    own_queries = projected[:, :, :head_dim].reshape(row_count, heads_dev * head_dim)
    gathered = lax.all_gather(own_queries, "blk", axis=0, tiled=True)
    prefix_keys = kv_cache[0].at[flagged].set(recomputed[:, :, :head_dim])
    prefix_values = kv_cache[1].at[flagged].set(recomputed[:, :, head_dim:])
    keys_all = jnp.concatenate([prefix_keys, projected[:, :, head_dim : 2 * head_dim]], axis=0)
    values_all = jnp.concatenate([prefix_values, projected[:, :, 2 * head_dim :]], axis=0)
    own_tenant = lax.dynamic_slice_in_dim(row_tenant, own_first, row_count, 0)
    key_tenant = jnp.concatenate([jnp.full((cache_rows,), block_tenant, jnp.int32), own_tenant])
    key_position = jnp.concatenate(
        [jnp.full((cache_rows,), -1, jnp.int32), own_first + jnp.arange(row_count, dtype=jnp.int32)]
    )
    scale = head_dim ** (-0.5)
    qblock = math.gcd(total_rows, 512)
    block_total = total_rows // qblock

    def partial_block(offset):
        query_block = lax.dynamic_slice_in_dim(gathered, offset, qblock, 0).reshape(
            qblock, heads_dev, head_dim
        )
        query_tenant = lax.dynamic_slice_in_dim(row_tenant, offset, qblock, 0)
        query_position = offset + jnp.arange(qblock, dtype=jnp.int32)
        allowed = (query_tenant[:, None] == key_tenant[None, :]) & (
            key_position[None, :] <= query_position[:, None]
        )
        scores = (
            jnp.einsum("qhd,khd->hqk", query_block, keys_all, preferred_element_type=jnp.float32)
            * scale
        )
        gate = allowed[None, :, :]
        row_peak = jnp.max(jnp.where(gate, scores, MASKED), axis=2)
        weights = jnp.where(gate, jnp.exp(scores - row_peak[:, :, None]), 0.0)
        denominator = jnp.sum(weights, axis=2)
        numerator = jnp.einsum(
            "hqk,khd->qhd",
            weights.astype(jnp.bfloat16),
            values_all,
            preferred_element_type=jnp.float32,
        )
        return (numerator.reshape(qblock, heads_dev * head_dim), denominator.T, row_peak.T)

    def fill_block(step_index, buffers):
        numer_buf, denom_buf, peak_buf = buffers
        offset = step_index * qblock
        numerator, denominator, row_peak = partial_block(offset)
        numer_buf = lax.dynamic_update_slice_in_dim(numer_buf, numerator, offset, 0)
        denom_buf = lax.dynamic_update_slice_in_dim(denom_buf, denominator, offset, 0)
        peak_buf = lax.dynamic_update_slice_in_dim(peak_buf, row_peak, offset, 0)
        return (numer_buf, denom_buf, peak_buf)

    initial = (
        jnp.zeros((total_rows, heads_dev * head_dim), jnp.float32),
        jnp.zeros((total_rows, heads_dev), jnp.float32),
        jnp.full((total_rows, heads_dev), MASKED, jnp.float32),
    )
    numer_buf, denom_buf, peak_buf = lax.fori_loop(0, block_total, fill_block, initial)
    width = heads_dev * head_dim + 2 * heads_dev
    packed = jnp.concatenate([numer_buf, denom_buf, peak_buf], axis=1).reshape(
        blk_total, row_count * width
    )
    received = lax.all_to_all(packed, "blk", split_axis=0, concat_axis=0, tiled=True)
    received = received.reshape(blk_total, row_count, width)
    recv_numer = received[:, :, : heads_dev * head_dim]
    recv_denom = received[:, :, heads_dev * head_dim : heads_dev * head_dim + heads_dev]
    recv_peak = received[:, :, heads_dev * head_dim + heads_dev :]
    best = jnp.max(recv_peak, axis=0)
    factor = jnp.exp(recv_peak - best[None])
    summed_denom = jnp.sum(factor * recv_denom, axis=0)
    summed_numer = jnp.sum(
        recv_numer.reshape(blk_total, row_count, heads_dev, head_dim) * factor[:, :, :, None],
        axis=0,
    )
    attended = (summed_numer / summed_denom[:, :, None]).astype(jnp.bfloat16)
    mixed = jnp.einsum("rhd,hde->re", attended, out_fetched, preferred_element_type=jnp.float32)
    head_total = lax.axis_size("head")
    columns = mixed.shape[1] // head_total
    pieces = mixed.astype(jnp.bfloat16).reshape(row_count, head_total, columns)
    pieces = jnp.transpose(pieces, (1, 0, 2))
    exchanged = lax.all_to_all(pieces, "head", split_axis=0, concat_axis=0, tiled=True)
    summed = jnp.sum(exchanged.astype(jnp.float32), axis=0)
    bias_part = lax.dynamic_slice_in_dim(out_bias, lax.axis_index("head") * columns, columns, 0)
    return (summed + bias_part).astype(jnp.bfloat16)


def solution(mesh):
    return jax.shard_map(
        body,
        mesh=mesh,
        in_specs=(
            P("blk", None),
            P("blk", None),
            P(None, "blk", "head", None),
            P(),
            P(),
            P("blk", "head", None),
            P("head", None),
            P("head", "blk", None),
            P(),
            P(),
            P(),
            P(),
            P("blk"),
        ),
        out_specs=P("blk", "head"),
        check_vma=False,
    )
```

```python
import math

import jax
import jax.numpy as jnp
from jax import lax
from jax.sharding import PartitionSpec as P

FLAG_DEV = 25
BLK = ("blk_hi", "blk_lo")


EPSILON = 1e-05
MASKED = -1e30


def layer_norm(states, norm_scale, norm_shift):
    widened = states.astype(jnp.float32)
    average = jnp.mean(widened, axis=-1, keepdims=True)
    center = widened - average
    variance = jnp.mean(center * center, axis=-1, keepdims=True)
    return (center * lax.rsqrt(variance + EPSILON) * norm_scale + norm_shift).astype(jnp.bfloat16)


def gather_blk(piece):
    inner = lax.all_gather(piece, "blk_lo", axis=0, tiled=True)
    return lax.all_gather(inner, "blk_hi", axis=0, tiled=True)


def body(
    suffix_hidden,
    prefix_hidden,
    kv_cache,
    norm_gain,
    norm_bias,
    qkv_weight,
    qkv_bias,
    out_weight,
    out_bias,
    suffix_lengths,
    prefix_blocks,
    block_owner,
    recompute_flag,
):
    blk_total = lax.axis_size(BLK)
    own_index = lax.axis_index(BLK)
    row_count = suffix_hidden.shape[0]
    cache_rows = prefix_hidden.shape[0]
    heads_dev = qkv_weight.shape[1]
    head_dim = qkv_weight.shape[2] // 3
    total_rows = row_count * blk_total
    own_first = own_index * row_count
    tenant_ends = jnp.cumsum(suffix_lengths)
    row_ids = jnp.arange(total_rows, dtype=jnp.int32)
    row_tenant = jnp.sum((row_ids[:, None] >= tenant_ends[None, :]).astype(jnp.int32), axis=1)
    block_ends = jnp.cumsum(prefix_blocks)
    block_slots = jnp.arange(blk_total, dtype=jnp.int32)
    global_block = jnp.sum(jnp.where(block_owner == own_index, block_slots, 0))
    block_tenant = jnp.sum((global_block >= block_ends).astype(jnp.int32))
    normed = layer_norm(suffix_hidden, norm_gain, norm_bias)
    flagged = jnp.argsort(1 - recompute_flag, stable=True)[:FLAG_DEV]
    prefix_normed = layer_norm(prefix_hidden[flagged], norm_gain, norm_bias)
    qkv_rows = qkv_weight.shape[0]
    out_rows = out_weight.shape[1]
    model_dim = out_weight.shape[2]
    out_lanes = heads_dev * out_rows * model_dim // qkv_rows
    packed_weights = jnp.concatenate(
        [
            qkv_weight.reshape(qkv_rows, heads_dev * 3 * head_dim),
            out_weight.reshape(qkv_rows, out_lanes),
        ],
        axis=1,
    )
    fetched_all = gather_blk(packed_weights)
    qkv_cols = heads_dev * 3 * head_dim
    fetched = fetched_all[:, :qkv_cols].reshape(blk_total * qkv_rows, heads_dev, 3 * head_dim)
    out_fetched = fetched_all[:, qkv_cols:].reshape(blk_total, heads_dev, out_rows, model_dim)
    out_fetched = jnp.transpose(out_fetched, (1, 0, 2, 3)).reshape(
        heads_dev, blk_total * out_rows, model_dim
    )
    piece_rows = fetched.shape[0]
    flattened = fetched.reshape(piece_rows, heads_dev * 3 * head_dim)
    kv_part = fetched[:, :, head_dim:].reshape(piece_rows, heads_dev * 2 * head_dim)
    suffix_acc = jnp.dot(normed, flattened, preferred_element_type=jnp.float32)
    prefix_acc = jnp.dot(prefix_normed, kv_part, preferred_element_type=jnp.float32)
    suffix_acc, prefix_acc = (suffix_acc, prefix_acc)
    projected = (
        (suffix_acc + qkv_bias.reshape(-1))
        .astype(jnp.bfloat16)
        .reshape(row_count, heads_dev, 3 * head_dim)
    )
    recomputed = (
        (prefix_acc + qkv_bias[:, head_dim:].reshape(-1))
        .astype(jnp.bfloat16)
        .reshape(FLAG_DEV, heads_dev, 2 * head_dim)
    )
    own_queries = projected[:, :, :head_dim].reshape(row_count, heads_dev * head_dim)
    gathered = gather_blk(own_queries)
    prefix_keys = kv_cache[0].at[flagged].set(recomputed[:, :, :head_dim])
    prefix_values = kv_cache[1].at[flagged].set(recomputed[:, :, head_dim:])
    keys_all = jnp.concatenate([prefix_keys, projected[:, :, head_dim : 2 * head_dim]], axis=0)
    values_all = jnp.concatenate([prefix_values, projected[:, :, 2 * head_dim :]], axis=0)
    own_tenant = lax.dynamic_slice_in_dim(row_tenant, own_first, row_count, 0)
    key_tenant = jnp.concatenate([jnp.full((cache_rows,), block_tenant, jnp.int32), own_tenant])
    key_position = jnp.concatenate(
        [jnp.full((cache_rows,), -1, jnp.int32), own_first + jnp.arange(row_count, dtype=jnp.int32)]
    )
    scale = head_dim ** (-0.5)
    qblock = math.gcd(total_rows, 512)
    block_total = total_rows // qblock

    def partial_block(offset):
        query_block = lax.dynamic_slice_in_dim(gathered, offset, qblock, 0).reshape(
            qblock, heads_dev, head_dim
        )
        query_tenant = lax.dynamic_slice_in_dim(row_tenant, offset, qblock, 0)
        query_position = offset + jnp.arange(qblock, dtype=jnp.int32)
        allowed = (query_tenant[:, None] == key_tenant[None, :]) & (
            key_position[None, :] <= query_position[:, None]
        )
        scores = (
            jnp.einsum("qhd,khd->hqk", query_block, keys_all, preferred_element_type=jnp.float32)
            * scale
        )
        gate = allowed[None, :, :]
        row_peak = jnp.max(jnp.where(gate, scores, MASKED), axis=2)
        weights = jnp.where(gate, jnp.exp(scores - row_peak[:, :, None]), 0.0)
        denominator = jnp.sum(weights, axis=2)
        numerator = jnp.einsum(
            "hqk,khd->qhd",
            weights.astype(jnp.bfloat16),
            values_all,
            preferred_element_type=jnp.float32,
        )
        return (numerator.reshape(qblock, heads_dev * head_dim), denominator.T, row_peak.T)

    def fill_block(step_index, buffers):
        numer_buf, denom_buf, peak_buf = buffers
        offset = step_index * qblock
        numerator, denominator, row_peak = partial_block(offset)
        numer_buf = lax.dynamic_update_slice_in_dim(numer_buf, numerator, offset, 0)
        denom_buf = lax.dynamic_update_slice_in_dim(denom_buf, denominator, offset, 0)
        peak_buf = lax.dynamic_update_slice_in_dim(peak_buf, row_peak, offset, 0)
        return (numer_buf, denom_buf, peak_buf)

    initial = (
        jnp.zeros((total_rows, heads_dev * head_dim), jnp.float32),
        jnp.zeros((total_rows, heads_dev), jnp.float32),
        jnp.full((total_rows, heads_dev), MASKED, jnp.float32),
    )
    numer_buf, denom_buf, peak_buf = lax.fori_loop(0, block_total, fill_block, initial)
    width = heads_dev * head_dim + 2 * heads_dev
    packed = jnp.concatenate([numer_buf, denom_buf, peak_buf], axis=1).reshape(
        blk_total, row_count * width
    )
    received = lax.all_to_all(packed, BLK, split_axis=0, concat_axis=0, tiled=True)
    received = received.reshape(blk_total, row_count, width)
    recv_numer = received[:, :, : heads_dev * head_dim]
    recv_denom = received[:, :, heads_dev * head_dim : heads_dev * head_dim + heads_dev]
    recv_peak = received[:, :, heads_dev * head_dim + heads_dev :]
    best = jnp.max(recv_peak, axis=0)
    factor = jnp.exp(recv_peak - best[None])
    summed_denom = jnp.sum(factor * recv_denom, axis=0)
    summed_numer = jnp.sum(
        recv_numer.reshape(blk_total, row_count, heads_dev, head_dim) * factor[:, :, :, None],
        axis=0,
    )
    attended = (summed_numer / summed_denom[:, :, None]).astype(jnp.bfloat16)
    mixed = jnp.einsum("rhd,hde->re", attended, out_fetched, preferred_element_type=jnp.float32)
    head_total = lax.axis_size("head")
    columns = mixed.shape[1] // head_total
    pieces = mixed.astype(jnp.bfloat16).reshape(row_count, head_total, columns)
    pieces = jnp.transpose(pieces, (1, 0, 2))
    exchanged = lax.all_to_all(pieces, "head", split_axis=0, concat_axis=0, tiled=True)
    summed = jnp.sum(exchanged.astype(jnp.float32), axis=0)
    bias_part = lax.dynamic_slice_in_dim(out_bias, lax.axis_index("head") * columns, columns, 0)
    return (summed + bias_part).astype(jnp.bfloat16)


def solution(mesh):
    blk_size = mesh.shape["blk"]
    blk_hi = math.isqrt(blk_size)
    while blk_size % blk_hi:
        blk_hi -= 1
    split = jax.sharding.Mesh(
        mesh.devices.reshape(mesh.shape["head"], blk_hi, blk_size // blk_hi),
        ("head", "blk_hi", "blk_lo"),
    )
    inner = jax.shard_map(
        body,
        mesh=split,
        in_specs=(
            P(BLK, None),
            P(BLK, None),
            P(None, BLK, "head", None),
            P(),
            P(),
            P(BLK, "head", None),
            P("head", None),
            P("head", BLK, None),
            P(),
            P(),
            P(),
            P(),
            P(BLK),
        ),
        out_specs=P(BLK, "head"),
        check_vma=False,
    )

    def run(*args):
        out = inner(*args)
        return jax.lax.with_sharding_constraint(
            out, jax.sharding.NamedSharding(mesh, P("blk", "head"))
        )

    return run
```
